32 devices in a mesh: station: 8 (over y, x, core), tm: 4 (over z).
Axes of the slice: x: 2, y: 2, z: 4, core: 2. Of those that a mesh axis runs over, the one named last changes fastest.
Arguments:
- samples: bfloat16 [64, 256, 2048], P('tm', 'station'), may hold values from -6 to 6
- history: bfloat16 [15, 256, 2048], P(None, 'station'), may hold values from -6 to 6
- taps: float32 [16, 2048], replicated, may hold values from -0.03125 to 0.03125
Outputs:
- visibility: float32 [1024, 2, 256, 256], P(('station', 'tm'))
- beam_power: float32 [64, 1024], P('tm', 'station')
The draws below stay inside these ranges and needn't reach their ends.
All inputs are finite; a program needn't handle non-finite values.
Results may differ from the reference program's by a relative error of at most 0.0095.
Values may be sent and summed in bfloat16 or wider, within the bound.
A program may use at most 128 MiB of HBM per device.

```python
import math
import jax
import jax.numpy as jnp
from jax import lax

STATIONS = 128
NCHAN = 1024
TAPS = 16
SPEC_DEV = 16
INPUTS = 256
NSPEC = 64
N_TM = 4


def levels(stream_key, extent, pieces, low, high):
    loudness = 1.0
    for axis_at, parts in pieces:
        draws = jax.random.uniform(jax.random.fold_in(jax.random.fold_in(stream_key, 6), axis_at), (parts,), jnp.float32, low / len(pieces), high / len(pieces))
        loudness = loudness * jnp.repeat(jnp.exp(draws), extent[axis_at] // parts).reshape((-1,) + (1,) * (len(extent) - 1 - axis_at))
    return loudness


def gaussian(own_key, shape, spread, most, split=(), kind=jnp.bfloat16):
    drawn = jax.random.normal(own_key, shape, jnp.float32) * spread
    if len(split) > 0:
        drawn = levels(own_key, shape, split, -0.22, 0.18) * drawn
    return jnp.clip(drawn, min=-most, max=most).astype(kind)


def setup_inputs(seed: int = 0) -> dict:
    key_list = jax.random.split(jax.random.key(seed), 4)
    samples = gaussian(key_list[0], (NSPEC, INPUTS, 2 * NCHAN), 1.0, 6.0, ((0, 4), (1, 8)))
    history = gaussian(key_list[1], (TAPS - 1, INPUTS, 2 * NCHAN), 1.0, 6.0, ((1, 8),))
    taps = gaussian(key_list[2], (TAPS, 2 * NCHAN), (TAPS * 2 * NCHAN) ** -0.5, 0.03125, (), jnp.float32)
    return dict(samples=samples, history=history, taps=taps)


def dft_table(frame_len, channels):
    sample_index = jnp.arange(frame_len, dtype=jnp.int32)
    channel_index = jnp.arange(channels, dtype=jnp.int32)
    phases = (sample_index[:, None] * channel_index[None, :]) % frame_len
    angles = phases.astype(jnp.float32) * (2.0 * math.pi / frame_len)
    dft_values = jnp.stack([jnp.cos(angles), -jnp.sin(angles)], axis=2)
    return dft_values.reshape(frame_len, 2 * channels).astype(jnp.bfloat16)


def filter_frames(extended, taps, frames_out):
    span_taps = taps.shape[0]
    running = jnp.zeros((frames_out,) + extended.shape[1:], jnp.float32)
    for tap_index in range(span_taps):
        offset = span_taps - 1 - tap_index
        running = running + taps[tap_index][None, None, :] * extended[offset:offset + frames_out].astype(jnp.float32)
    return running.astype(jnp.bfloat16)


def beam_power_of(spectra):
    values = spectra.astype(jnp.float32)
    return jnp.sum(values * values, axis=(1, 3)) * (1.0 / spectra.shape[1])


def correlate(spectra, norm_scale):
    values = spectra.astype(jnp.float32)
    rotated = jnp.stack([-values[..., 1], values[..., 0]], axis=-1)
    real_part = jnp.einsum('tacp,tbcp->cab', values, values, precision=lax.Precision.HIGHEST) * norm_scale
    imag_part = jnp.einsum('tacp,tbcp->cab', rotated, values, precision=lax.Precision.HIGHEST) * norm_scale
    return real_part, imag_part


def reference(samples, history, taps):
    frame_len = 2 * NCHAN
    inputs = 2 * STATIONS
    dft_values = dft_table(frame_len, NCHAN).astype(jnp.float32)
    norm_scale = 1.0 / (SPEC_DEV * N_TM)
    blocks = samples.reshape(N_TM, SPEC_DEV, inputs, frame_len)

    def advance(state_pair, time_block):
        prior_frames, running = state_pair
        extended = jnp.concatenate([prior_frames, time_block], axis=0)
        weighted = filter_frames(extended, taps, SPEC_DEV)
        weighted = lax.optimization_barrier(weighted)
        spectra = jnp.dot(weighted.reshape(SPEC_DEV * inputs, frame_len).astype(jnp.float32), dft_values,
                          precision=lax.Precision.HIGHEST, preferred_element_type=jnp.float32)
        spectra = lax.optimization_barrier(spectra.astype(jnp.bfloat16))
        spectra = spectra.reshape(SPEC_DEV, inputs, NCHAN, 2)
        power_rows = beam_power_of(spectra)
        real_part, imag_part = correlate(spectra, norm_scale)
        partial_value = jnp.stack([real_part, imag_part], axis=1).astype(jnp.bfloat16)
        partial_value = lax.optimization_barrier(partial_value)
        running = running + partial_value.astype(jnp.float32)
        return (time_block[SPEC_DEV - (TAPS - 1):], running), power_rows

    initial_sum = jnp.zeros((NCHAN, 2, inputs, inputs), jnp.float32)
    final_pair, powers = lax.scan(advance, (history, initial_sum), blocks)
    return final_pair[1], powers.reshape(SPEC_DEV * N_TM, NCHAN)
```

```python
import functools
import math

import jax
import jax.numpy as jnp
from jax import lax
from jax.experimental import pallas as pl
from jax.experimental.pallas import tpu as pltpu
from jax.sharding import PartitionSpec as P

BOTH = ("station", "tm")
VMEM_LIMIT = 56 * 1024 * 1024


def passed_along(block, axis, distance):
    devices = range(lax.axis_size(axis))
    route = [(i - distance, i) for i in devices if i - distance in devices]
    return lax.ppermute(block, axis, route)


def angle_tables(rows, step, frame_len):
    row = jnp.arange(rows, dtype=jnp.int32) * step
    sample = jnp.arange(frame_len, dtype=jnp.int32)
    phases = row[:, None] * sample[None, :] % frame_len
    angles = phases.astype(jnp.float32) * (2.0 * math.pi / frame_len)
    return jnp.cos(angles), jnp.sin(angles)


def filter_frames(extended, taps, frames_out):
    span_taps = taps.shape[0]
    running = jnp.zeros((frames_out,) + extended.shape[1:], jnp.float32)
    for tap_index in range(span_taps):
        offset = span_taps - 1 - tap_index
        running = running + taps[tap_index][None, None, :] * extended[
            offset : offset + frames_out
        ].astype(jnp.float32)
    return running.astype(jnp.bfloat16)


def dft_kernel(own, cos_hi, sin_hi, cos_lo, sin_lo, weighted, pick, spec, power, table):
    group = cos_hi.shape[0]
    c_lo, s_lo = cos_lo[...], sin_lo[...]
    for g in range(group):
        c_hi, s_hi = cos_hi[g : g + 1], sin_hi[g : g + 1]
        real = c_hi * c_lo - s_hi * s_lo
        imag = -(s_hi * c_lo + c_hi * s_lo)
        table[g * 2 * own : (g + 1) * 2 * own] = jnp.concatenate([real, imag], axis=0).astype(
            jnp.bfloat16
        )
    out = lax.dot_general(
        table[...], weighted[...], (((1,), (1,)), ((), ())), preferred_element_type=jnp.float32
    )
    out = out.astype(jnp.bfloat16).reshape(group, 2 * own, out.shape[1])
    spec[...] = out
    values = out.astype(jnp.float32)
    values = values * values
    total = (values[:, :own] + values[:, own:]).reshape(group * own, out.shape[2])
    power[...] = lax.dot_general(
        pick[...],
        total,
        (((1,), (1,)), ((), ())),
        precision=lax.Precision.HIGHEST,
        preferred_element_type=jnp.float32,
    )


def channelise(weighted, own, frames, dests):
    rows, frame_len = weighted.shape
    group = max(1, min(dests, 512 // (2 * own)))
    cos_hi, sin_hi = angle_tables(dests, own, frame_len)
    cos_lo, sin_lo = angle_tables(own, 1, frame_len)
    column = jnp.arange(rows, dtype=jnp.int32) // (rows // frames)
    pick = (column[None, :] == jnp.arange(frames, dtype=jnp.int32)[:, None]).astype(jnp.float32)
    whole = lambda a: pl.BlockSpec(a.shape, lambda i: (0, 0))
    high = pl.BlockSpec((group, frame_len), lambda i: (i, 0))
    return pl.pallas_call(
        functools.partial(dft_kernel, own),
        grid=(dests // group,),
        in_specs=[high, high, whole(cos_lo), whole(sin_lo), whole(weighted), whole(pick)],
        out_specs=[
            pl.BlockSpec((group, 2 * own, rows), lambda i: (i, 0, 0)),
            pl.BlockSpec((frames, group * own), lambda i: (0, i)),
        ],
        out_shape=[
            jax.ShapeDtypeStruct((dests, 2 * own, rows), jnp.bfloat16),
            jax.ShapeDtypeStruct((frames, dests * own), jnp.float32),
        ],
        scratch_shapes=[pltpu.VMEM((group * 2 * own, frame_len), jnp.bfloat16)],
        compiler_params=pltpu.CompilerParams(vmem_limit_bytes=VMEM_LIMIT),
    )(cos_hi, sin_hi, cos_lo, sin_lo, weighted, pick)


def correlate_kernel(stations, blocks, own, local, scale, got, vis, wide):
    chunks = got.shape[2] // 128
    slots = 128 // local
    channel = pl.program_id(0)

    @pl.when(channel == 0)
    def _():
        def fill(s, carry):
            for tm in range(blocks):
                for p in range(2):
                    piece = got[s * blocks + tm, p * own : (p + 1) * own, :].astype(jnp.float32)
                    base = (p * blocks + tm) * own
                    for j in range(chunks):
                        wide[s * chunks + j, base : base + own, :] = piece[
                            :, j * 128 : (j + 1) * 128
                        ]
            return carry

        lax.fori_loop(0, stations, fill, 0)

    rows = 2 * blocks
    lane = lax.broadcasted_iota(jnp.int32, (rows, 128), 1) // local
    sign = jnp.where(lax.broadcasted_iota(jnp.int32, (rows, 256), 0) < blocks, 1.0, -1.0)
    flat, turned = [], []
    for j in range(chunks):
        halves = []
        for h in range(stations // slots):
            parts = [
                wide[(h * slots + s) * chunks + j, pl.ds(channel, rows, stride=own), :]
                for s in range(slots)
            ]
            tiles = []
            for t in range(slots):
                tile = None
                for s in range(slots):
                    shift = (s - t) % slots * local
                    moved = parts[s] if shift == 0 else pltpu.roll(parts[s], shift, 1)
                    tile = moved if tile is None else jnp.where(lane == s, moved, tile)
                tiles.append(tile)
            halves.append(tiles)
        for t in range(slots):
            full = jnp.concatenate([half[t] for half in halves], axis=1)
            flat.append(full)
            turned.append(pltpu.roll(full, blocks, 0) * sign)
    flat = jnp.concatenate(flat, axis=0).astype(jnp.bfloat16)
    turned = jnp.concatenate(turned, axis=0).astype(jnp.bfloat16)
    over_rows = (((0,), (0,)), ((), ()))
    vis[0, 0] = lax.dot_general(flat, flat, over_rows, preferred_element_type=jnp.float32) * scale
    vis[0, 1] = lax.dot_general(flat, turned, over_rows, preferred_element_type=jnp.float32) * scale


def correlate(got, stations, blocks, own, local, scale):
    inputs = stations * local
    chunks = got.shape[2] // 128
    return pl.pallas_call(
        functools.partial(correlate_kernel, stations, blocks, own, local, scale),
        grid=(own,),
        in_specs=[pl.BlockSpec(got.shape, lambda c: (0, 0, 0))],
        out_specs=pl.BlockSpec((1, 2, inputs, inputs), lambda c: (c, 0, 0, 0)),
        out_shape=jax.ShapeDtypeStruct((own, 2, inputs, inputs), jnp.float32),
        scratch_shapes=[pltpu.VMEM((stations * chunks, 2 * blocks * own, 128), jnp.float32)],
        compiler_params=pltpu.CompilerParams(vmem_limit_bytes=VMEM_LIMIT),
    )(got)


def body(samples, history, taps):
    frames_dev, local, frame_len = samples.shape
    span_taps = taps.shape[0]
    stations, blocks = lax.axis_size("station"), lax.axis_size("tm")
    dests = stations * blocks
    own = frame_len // 2 // dests
    tail_block = samples[frames_dev - (span_taps - 1) :]
    prior_frames = passed_along(tail_block, "tm", 1)
    prior_frames = jnp.where(lax.axis_index("tm") == 0, history, prior_frames)
    extended = jnp.concatenate([prior_frames, samples], axis=0)
    weighted = filter_frames(extended, taps, frames_dev).reshape(frames_dev * local, frame_len)
    spectra, power = channelise(weighted, own, frames_dev, dests)
    got = lax.all_to_all(spectra, BOTH, split_axis=0, concat_axis=0, tiled=True)
    power = lax.psum_scatter(power, "station", scatter_dimension=1, tiled=True)
    power = power * (1.0 / (stations * local))
    visibility = correlate(got, stations, blocks, own, local, 1.0 / (frames_dev * blocks))
    return visibility, power


def solution(mesh):
    return jax.shard_map(
        body,
        mesh=mesh,
        in_specs=(P("tm", "station", None), P(None, "station", None), P()),
        out_specs=(P(("station", "tm"), None, None, None), P("tm", "station")),
        check_vma=False,
    )
```

```python
import functools
import math

import jax
import jax.numpy as jnp
from jax import lax
from jax.experimental import pallas as pl
from jax.experimental.pallas import tpu as pltpu
from jax.sharding import PartitionSpec as P

BOTH = ("station", "tm")
VMEM_LIMIT = 56 * 1024 * 1024


def passed_along(block, axis, distance):
    devices = range(lax.axis_size(axis))
    route = [(i - distance, i) for i in devices if i - distance in devices]
    return lax.ppermute(block, axis, route)


def angle_tables(rows, step, frame_len):
    row = jnp.arange(rows, dtype=jnp.int32) * step
    sample = jnp.arange(frame_len, dtype=jnp.int32)
    phases = row[:, None] * sample[None, :] % frame_len
    angles = phases.astype(jnp.float32) * (2.0 * math.pi / frame_len)
    return jnp.cos(angles), jnp.sin(angles)


def filter_frames(extended, taps, frames_out):
    span_taps = taps.shape[0]
    running = jnp.zeros((frames_out,) + extended.shape[1:], jnp.float32)
    for tap_index in range(span_taps):
        offset = span_taps - 1 - tap_index
        running = running + taps[tap_index][None, None, :] * extended[
            offset : offset + frames_out
        ].astype(jnp.float32)
    return running.astype(jnp.bfloat16)


def table_kernel(own, cos_hi, sin_hi, cos_lo, sin_lo, table):
    c_lo, s_lo = cos_lo[...], sin_lo[...]
    for g in range(cos_hi.shape[0]):
        c_hi, s_hi = cos_hi[g : g + 1], sin_hi[g : g + 1]
        real = c_hi * c_lo - s_hi * s_lo
        imag = -(s_hi * c_lo + c_hi * s_lo)
        table[g * 2 * own : (g + 1) * 2 * own] = jnp.concatenate([real, imag], axis=0).astype(
            jnp.bfloat16
        )


def dft_table(own, dests, group, frame_len):
    cos_hi, sin_hi = angle_tables(dests, own, frame_len)
    cos_lo, sin_lo = angle_tables(own, 1, frame_len)
    high = pl.BlockSpec((group, frame_len), lambda i: (i, 0))
    low = pl.BlockSpec((own, frame_len), lambda i: (0, 0))
    return pl.pallas_call(
        functools.partial(table_kernel, own),
        grid=(dests // group,),
        in_specs=[high, high, low, low],
        out_specs=pl.BlockSpec((group * 2 * own, frame_len), lambda i: (i, 0)),
        out_shape=jax.ShapeDtypeStruct((dests * 2 * own, frame_len), jnp.bfloat16),
        compiler_params=pltpu.CompilerParams(vmem_limit_bytes=VMEM_LIMIT),
        cost_estimate=pl.CostEstimate(
            flops=dests * own * frame_len * 8,
            bytes_accessed=dests * own * frame_len * 4,
            transcendentals=0,
        ),
    )(cos_hi, sin_hi, cos_lo, sin_lo)


def dft_kernel(own, table, weighted, pick, spec, power):
    group = spec.shape[0]
    out = lax.dot_general(
        table[...], weighted[...], (((1,), (1,)), ((), ())), preferred_element_type=jnp.float32
    )
    out = out.astype(jnp.bfloat16).reshape(group, 2 * own, out.shape[1])
    spec[...] = out
    values = out.astype(jnp.float32)
    values = values * values
    total = (values[:, :own] + values[:, own:]).reshape(group * own, out.shape[2])
    power[...] = lax.dot_general(
        pick[...],
        total,
        (((1,), (1,)), ((), ())),
        precision=lax.Precision.HIGHEST,
        preferred_element_type=jnp.float32,
    )


def channelise(table, weighted, own, frames, dests, group):
    rows, frame_len = weighted.shape
    column = jnp.arange(rows, dtype=jnp.int32) // (rows // frames)
    pick = (column[None, :] == jnp.arange(frames, dtype=jnp.int32)[:, None]).astype(jnp.float32)
    return pl.pallas_call(
        functools.partial(dft_kernel, own),
        grid=(dests // group,),
        in_specs=[
            pl.BlockSpec((group * 2 * own, frame_len), lambda i: (i, 0)),
            pl.BlockSpec((rows, frame_len), lambda i: (0, 0)),
            pl.BlockSpec((frames, rows), lambda i: (0, 0)),
        ],
        out_specs=[
            pl.BlockSpec((group, 2 * own, rows), lambda i: (i, 0, 0)),
            pl.BlockSpec((frames, group * own), lambda i: (0, i)),
        ],
        out_shape=[
            jax.ShapeDtypeStruct((dests, 2 * own, rows), jnp.bfloat16),
            jax.ShapeDtypeStruct((frames, dests * own), jnp.float32),
        ],
        compiler_params=pltpu.CompilerParams(vmem_limit_bytes=VMEM_LIMIT),
        cost_estimate=pl.CostEstimate(
            flops=4 * dests * own * frame_len * rows,
            bytes_accessed=dests * own * frame_len * 4,
            transcendentals=0,
        ),
    )(table, weighted, pick)


def channel_rows(wide, channel, stations, blocks, own, local):
    chunks = wide.shape[0] // stations
    slots = 128 // local
    rows = 2 * blocks
    lane = lax.broadcasted_iota(jnp.int32, (rows, 128), 1) // local
    sign = jnp.where(
        lax.broadcasted_iota(jnp.int32, (rows, stations * local), 0) < blocks, 1.0, -1.0
    )
    flat, turned = [], []
    for j in range(chunks):
        halves = []
        for h in range(stations // slots):
            parts = [
                wide[(h * slots + s) * chunks + j, pl.ds(channel, rows, stride=own), :]
                for s in range(slots)
            ]
            tiles = []
            for t in range(slots):
                tile = None
                for s in range(slots):
                    shift = (s - t) % slots * local
                    moved = parts[s] if shift == 0 else pltpu.roll(parts[s], shift, 1)
                    tile = moved if tile is None else jnp.where(lane == s, moved, tile)
                tiles.append(tile)
            halves.append(tiles)
        for t in range(slots):
            full = jnp.concatenate([half[t] for half in halves], axis=1)
            flat.append(full)
            turned.append(pltpu.roll(full, blocks, 0) * sign)
    flat = jnp.concatenate(flat, axis=0).astype(jnp.bfloat16)
    turned = jnp.concatenate(turned, axis=0).astype(jnp.bfloat16)
    return flat, turned


def correlate_kernel(stations, blocks, own, local, scale, *refs):
    *parts, vis, wide = refs
    chunks = parts[0].shape[2] // 128
    group = vis.shape[0]
    inputs = stations * local
    step = pl.program_id(0)

    @pl.when(step == 0)
    def _():
        def fill(s, carry):
            for i, got in enumerate(parts):
                for tm in range(blocks):
                    for p in range(2):
                        piece = got[s * blocks + tm, p * own : (p + 1) * own, :]
                        piece = piece.astype(jnp.float32)
                        base = (p * blocks + tm) * own
                        for j in range(chunks):
                            at = (s * len(parts) + i) * chunks + j
                            wide[at, base : base + own, :] = piece[:, j * 128 : (j + 1) * 128]
            return carry

        lax.fori_loop(0, stations, fill, 0)

    for g in range(group):
        flat, turned = channel_rows(wide, step * group + g, stations, blocks, own, local)
        both = jnp.concatenate([flat, turned], axis=1)
        out = lax.dot_general(
            flat, both, (((0,), (0,)), ((), ())), preferred_element_type=jnp.float32
        )
        vis[g, 0] = out[:, :inputs] * scale
        vis[g, 1] = out[:, inputs:] * scale


def correlate(parts, stations, blocks, own, local, scale):
    inputs = stations * local
    chunks = sum(got.shape[2] for got in parts) // 128
    group = math.gcd(own, 4)
    return pl.pallas_call(
        functools.partial(correlate_kernel, stations, blocks, own, local, scale),
        grid=(own // group,),
        in_specs=[pl.BlockSpec(got.shape, lambda c: (0, 0, 0)) for got in parts],
        out_specs=pl.BlockSpec((group, 2, inputs, inputs), lambda c: (c, 0, 0, 0)),
        out_shape=jax.ShapeDtypeStruct((own, 2, inputs, inputs), jnp.float32),
        scratch_shapes=[pltpu.VMEM((stations * chunks, 2 * blocks * own, 128), jnp.float32)],
        compiler_params=pltpu.CompilerParams(vmem_limit_bytes=VMEM_LIMIT),
    )(*parts)


def body(samples, history, taps):
    frames_dev, local, frame_len = samples.shape
    span = taps.shape[0] - 1
    stations, blocks = lax.axis_size("station"), lax.axis_size("tm")
    dests = stations * blocks
    own = frame_len // 2 // dests
    group = max(1, min(dests, 512 // (2 * own)))
    half = frames_dev // 2
    first = lax.axis_index("tm") == 0
    tail = samples[frames_dev - span :]

    near = passed_along(tail[half:], "tm", 1)
    table = dft_table(own, dests, group, frame_len)
    near, far_tail, table = lax.optimization_barrier((near, tail[:half], table))
    far = passed_along(far_tail, "tm", 1)
    near = jnp.where(first, history[half:], near)
    late = filter_frames(jnp.concatenate([near, samples], axis=0), taps, half)
    late = late.reshape(half * local, frame_len)
    spec_late, power_late = channelise(table, late, own, half, dests, group)
    got_late = lax.all_to_all(spec_late, BOTH, split_axis=0, concat_axis=0, tiled=True)

    far = jnp.where(first, history[:half], far)
    early = filter_frames(jnp.concatenate([far, near, samples[:half]], axis=0), taps, half)
    early = early.reshape(half * local, frame_len)
    spec_early, power_early = channelise(table, early, own, half, dests, group)
    got_early = lax.all_to_all(spec_early, BOTH, split_axis=0, concat_axis=0, tiled=True)

    power = jnp.concatenate([power_early, power_late], axis=0)
    power = lax.psum_scatter(power, "station", scatter_dimension=1, tiled=True)
    power = power * (1.0 / (stations * local))
    scale = 1.0 / (frames_dev * blocks)
    visibility = correlate((got_early, got_late), stations, blocks, own, local, scale)
    return visibility, power


def solution(mesh):
    return jax.shard_map(
        body,
        mesh=mesh,
        in_specs=(P("tm", "station", None), P(None, "station", None), P()),
        out_specs=(P(("station", "tm"), None, None, None), P("tm", "station")),
        check_vma=False,
    )
```

```python
import functools
import math

import jax
import jax.numpy as jnp
from jax import lax
from jax.experimental import pallas as pl
from jax.experimental.pallas import tpu as pltpu
from jax.sharding import PartitionSpec as P

BOTH = ("station", "tm")
VMEM_LIMIT = 24 * 1024 * 1024


def passed_along(block, axis, distance):
    devices = range(lax.axis_size(axis))
    route = [(i - distance, i) for i in devices if i - distance in devices]
    return lax.ppermute(block, axis, route)


def angle_tables(rows, step, frame_len):
    row = jnp.arange(rows, dtype=jnp.int32) * step
    sample = jnp.arange(frame_len, dtype=jnp.int32)
    phases = row[:, None] * sample[None, :] % frame_len
    angles = phases.astype(jnp.float32) * (2.0 * math.pi / frame_len)
    return jnp.cos(angles), jnp.sin(angles)


def filter_frames(extended, taps, frames_out):
    span_taps = taps.shape[0]
    running = jnp.zeros((frames_out,) + extended.shape[1:], jnp.float32)
    for tap_index in range(span_taps):
        offset = span_taps - 1 - tap_index
        running = running + taps[tap_index][None, None, :] * extended[
            offset : offset + frames_out
        ].astype(jnp.float32)
    return running.astype(jnp.bfloat16)


def table_kernel(own, cos_hi, sin_hi, cos_lo, sin_lo, table):
    c_lo, s_lo = cos_lo[...], sin_lo[...]
    for g in range(cos_hi.shape[0]):
        c_hi, s_hi = cos_hi[g : g + 1], sin_hi[g : g + 1]
        real = c_hi * c_lo - s_hi * s_lo
        imag = -(s_hi * c_lo + c_hi * s_lo)
        table[g * 2 * own : (g + 1) * 2 * own] = jnp.concatenate([real, imag], axis=0).astype(
            jnp.bfloat16
        )


def dft_table(own, dests, group, frame_len):
    cos_hi, sin_hi = angle_tables(dests, own, frame_len)
    cos_lo, sin_lo = angle_tables(own, 1, frame_len)
    high = pl.BlockSpec((group, frame_len), lambda i: (i, 0))
    low = pl.BlockSpec((own, frame_len), lambda i: (0, 0))
    return pl.pallas_call(
        functools.partial(table_kernel, own),
        grid=(dests // group,),
        in_specs=[high, high, low, low],
        out_specs=pl.BlockSpec((group * 2 * own, frame_len), lambda i: (i, 0)),
        out_shape=jax.ShapeDtypeStruct((dests * 2 * own, frame_len), jnp.bfloat16),
        compiler_params=pltpu.CompilerParams(vmem_limit_bytes=VMEM_LIMIT),
        cost_estimate=pl.CostEstimate(
            flops=dests * own * frame_len * 8,
            bytes_accessed=dests * own * frame_len * 4,
            transcendentals=0,
        ),
    )(cos_hi, sin_hi, cos_lo, sin_lo)


def dft_kernel(own, table, weighted, pick, spec, power):
    group = spec.shape[0]
    out = lax.dot_general(
        table[...], weighted[...], (((1,), (1,)), ((), ())), preferred_element_type=jnp.float32
    )
    out = out.astype(jnp.bfloat16).reshape(group, 2 * own, out.shape[1])
    spec[...] = out
    values = out.astype(jnp.float32)
    values = values * values
    total = (values[:, :own] + values[:, own:]).reshape(group * own, out.shape[2])
    power[...] = lax.dot_general(
        pick[...],
        total,
        (((1,), (1,)), ((), ())),
        precision=lax.Precision.HIGHEST,
        preferred_element_type=jnp.float32,
    )


def channelise(table, weighted, own, frames, dests, group):
    rows, frame_len = weighted.shape
    column = jnp.arange(rows, dtype=jnp.int32) // (rows // frames)
    pick = (column[None, :] == jnp.arange(frames, dtype=jnp.int32)[:, None]).astype(jnp.float32)
    return pl.pallas_call(
        functools.partial(dft_kernel, own),
        grid=(dests // group,),
        in_specs=[
            pl.BlockSpec((group * 2 * own, frame_len), lambda i: (i, 0)),
            pl.BlockSpec((rows, frame_len), lambda i: (0, 0)),
            pl.BlockSpec((frames, rows), lambda i: (0, 0)),
        ],
        out_specs=[
            pl.BlockSpec((group, 2 * own, rows), lambda i: (i, 0, 0)),
            pl.BlockSpec((frames, group * own), lambda i: (0, i)),
        ],
        out_shape=[
            jax.ShapeDtypeStruct((dests, 2 * own, rows), jnp.bfloat16),
            jax.ShapeDtypeStruct((frames, dests * own), jnp.float32),
        ],
        compiler_params=pltpu.CompilerParams(vmem_limit_bytes=VMEM_LIMIT),
        cost_estimate=pl.CostEstimate(
            flops=4 * dests * own * frame_len * rows,
            bytes_accessed=dests * own * frame_len * 4,
            transcendentals=0,
        ),
    )(table, weighted, pick)


def channel_rows(wide, channel, stations, blocks, own, local):
    chunks = wide.shape[0] // stations
    slots = 128 // local
    rows = 2 * blocks
    lane = lax.broadcasted_iota(jnp.int32, (rows, 128), 1) // local
    sign = jnp.where(
        lax.broadcasted_iota(jnp.int32, (rows, stations * local), 0) < blocks, 1.0, -1.0
    )
    flat, turned = [], []
    for j in range(chunks):
        halves = []
        for h in range(stations // slots):
            parts = [
                wide[(h * slots + s) * chunks + j, pl.ds(channel, rows, stride=own), :]
                for s in range(slots)
            ]
            tiles = []
            for t in range(slots):
                tile = None
                for s in range(slots):
                    shift = (s - t) % slots * local
                    moved = parts[s] if shift == 0 else pltpu.roll(parts[s], shift, 1)
                    tile = moved if tile is None else jnp.where(lane == s, moved, tile)
                tiles.append(tile)
            halves.append(tiles)
        for t in range(slots):
            full = jnp.concatenate([half[t] for half in halves], axis=1)
            flat.append(full)
            turned.append(pltpu.roll(full, blocks, 0) * sign)
    flat = jnp.concatenate(flat, axis=0).astype(jnp.bfloat16)
    turned = jnp.concatenate(turned, axis=0).astype(jnp.bfloat16)
    return flat, turned


def spread(got, wide, stations, blocks, own):
    chunks = got.shape[2] // 128

    def fill(s, carry):
        for tm in range(blocks):
            for p in range(2):
                piece = got[s * blocks + tm, p * own : (p + 1) * own, :].astype(jnp.float32)
                base = (p * blocks + tm) * own
                for j in range(chunks):
                    wide[s * chunks + j, base : base + own, :] = piece[:, j * 128 : (j + 1) * 128]
        return carry

    lax.fori_loop(0, stations, fill, 0)


def arrange_kernel(stations, blocks, own, local, got, both, wide):
    step = pl.program_id(0)
    group = both.shape[0]
    pl.when(step == 0)(lambda: spread(got, wide, stations, blocks, own))
    for g in range(group):
        pair = channel_rows(wide, step * group + g, stations, blocks, own, local)
        both[g] = jnp.concatenate(pair, axis=1)


def correlate_kernel(stations, blocks, own, local, scale, got, late, vis, wide):
    step = pl.program_id(0)
    group = vis.shape[0]
    inputs = stations * local
    pl.when(step == 0)(lambda: spread(got, wide, stations, blocks, own))
    for g in range(group):
        pair = channel_rows(wide, step * group + g, stations, blocks, own, local)
        both = jnp.concatenate([jnp.concatenate(pair, axis=1), late[g]], axis=0)
        out = lax.dot_general(
            both[:, :inputs],
            both,
            (((0,), (0,)), ((), ())),
            preferred_element_type=jnp.float32,
        )
        vis[g, 0] = out[:, :inputs] * scale
        vis[g, 1] = out[:, inputs:] * scale


def arrange(got, stations, blocks, own, local):
    inputs = stations * local
    depth = got.shape[2] // local * blocks * 2
    group = math.gcd(own, 4)
    return pl.pallas_call(
        functools.partial(arrange_kernel, stations, blocks, own, local),
        grid=(own // group,),
        in_specs=[pl.BlockSpec(memory_space=pltpu.VMEM)],
        out_specs=pl.BlockSpec((group, depth, 2 * inputs), lambda c: (c, 0, 0)),
        out_shape=jax.ShapeDtypeStruct((own, depth, 2 * inputs), jnp.bfloat16),
        scratch_shapes=[
            pltpu.VMEM((stations * got.shape[2] // 128, 2 * blocks * own, 128), jnp.float32)
        ],
        compiler_params=pltpu.CompilerParams(vmem_limit_bytes=VMEM_LIMIT),
        cost_estimate=pl.CostEstimate(
            flops=got.size * 100, bytes_accessed=got.size * 12, transcendentals=0
        ),
    )(got)


def correlate(got, late, stations, blocks, own, local, scale):
    inputs = stations * local
    group = math.gcd(own, 4)
    return pl.pallas_call(
        functools.partial(correlate_kernel, stations, blocks, own, local, scale),
        grid=(own // group,),
        in_specs=[
            pl.BlockSpec(memory_space=pltpu.VMEM),
            pl.BlockSpec((group,) + late.shape[1:], lambda c: (c, 0, 0)),
        ],
        out_specs=pl.BlockSpec((group, 2, inputs, inputs), lambda c: (c, 0, 0, 0)),
        out_shape=jax.ShapeDtypeStruct((own, 2, inputs, inputs), jnp.float32),
        scratch_shapes=[
            pltpu.VMEM((stations * got.shape[2] // 128, 2 * blocks * own, 128), jnp.float32)
        ],
        compiler_params=pltpu.CompilerParams(vmem_limit_bytes=VMEM_LIMIT),
    )(got, late)


def sum_scatter(rows):
    count = rows.shape[0]
    me = lax.axis_index("station")
    distance = count // 2
    while distance > 0:
        upper = me // distance % 2 == 1
        low, high = rows[:distance], rows[distance:]
        route = [(i, i ^ distance) for i in range(count)]
        other = lax.ppermute(jnp.where(upper, low, high), "station", route)
        rows = jnp.where(upper, high, low) + other
        distance //= 2
    return rows[0]


def body(samples, history, taps):
    frames_dev, local, frame_len = samples.shape
    span = taps.shape[0] - 1
    stations, blocks = lax.axis_size("station"), lax.axis_size("tm")
    dests = stations * blocks
    own = frame_len // 2 // dests
    group = max(1, min(dests, 512 // (2 * own)))
    half = frames_dev // 2
    first = lax.axis_index("tm") == 0
    tail = samples[frames_dev - span :]

    near = passed_along(tail[half:], "tm", 1)
    table = dft_table(own, dests, group, frame_len)
    near, far_tail, table = lax.optimization_barrier((near, tail[:half], table))
    far = passed_along(far_tail, "tm", 1)
    near = jnp.where(first, history[half:], near)
    late = filter_frames(jnp.concatenate([near, samples], axis=0), taps, half)
    late = late.reshape(half * local, frame_len)
    spec_late, power_late = channelise(table, late, own, half, dests, group)
    got_late = lax.all_to_all(spec_late, BOTH, split_axis=0, concat_axis=0, tiled=True)

    far = jnp.where(first, history[:half], far)
    early = filter_frames(jnp.concatenate([far, near, samples[:half]], axis=0), taps, half)
    early = early.reshape(half * local, frame_len)
    spec_early, power_early = channelise(table, early, own, half, dests, group)
    got_late, spec_early, power_early = lax.optimization_barrier(
        (got_late, spec_early, power_early)
    )
    got_early = lax.all_to_all(spec_early, BOTH, split_axis=0, concat_axis=0, tiled=True)

    power = jnp.concatenate([power_early, power_late], axis=0)
    power = sum_scatter(power.reshape(frames_dev, stations, blocks * own).transpose(1, 0, 2))
    power = power * (1.0 / (stations * local))
    scale = 1.0 / (frames_dev * blocks)
    arranged = arrange(got_late, stations, blocks, own, local)
    visibility = correlate(got_early, arranged, stations, blocks, own, local, scale)
    return visibility, power


def solution(mesh):
    return jax.shard_map(
        body,
        mesh=mesh,
        in_specs=(P("tm", "station", None), P(None, "station", None), P()),
        out_specs=(P(("station", "tm"), None, None, None), P("tm", "station")),
        check_vma=False,
    )
```

```python
import functools
import math

import jax
import jax.numpy as jnp
from jax import lax
from jax.experimental import pallas as pl
from jax.experimental.pallas import tpu as pltpu
from jax.sharding import PartitionSpec as P

BOTH = ("station", "tm")
VMEM_LIMIT = 14 * 1024 * 1024


def passed_along(block, axis, distance):
    devices = range(lax.axis_size(axis))
    route = [(i - distance, i) for i in devices if i - distance in devices]
    return lax.ppermute(block, axis, route)


def angle_tables(rows, step, frame_len):
    row = jnp.arange(rows, dtype=jnp.int32) * step
    sample = jnp.arange(frame_len, dtype=jnp.int32)
    phases = row[:, None] * sample[None, :] % frame_len
    angles = phases.astype(jnp.float32) * (2.0 * math.pi / frame_len)
    return jnp.cos(angles), jnp.sin(angles)


def filter_frames(extended, taps, frames_out, first_tap=0):
    span_taps = taps.shape[0]
    running = jnp.zeros((frames_out,) + extended.shape[1:], jnp.float32)
    for tap_index in range(first_tap, span_taps):
        offset = span_taps - 1 - tap_index
        running = running + taps[tap_index][None, None, :] * extended[
            offset : offset + frames_out
        ].astype(jnp.float32)
    return running


def padded(frames, before, after):
    return jnp.pad(frames, ((before, after), (0, 0), (0, 0)))


def table_kernel(own, cos_hi, sin_hi, cos_lo, sin_lo, table):
    c_lo, s_lo = cos_lo[...], sin_lo[...]
    for g in range(cos_hi.shape[0]):
        c_hi, s_hi = cos_hi[g : g + 1], sin_hi[g : g + 1]
        real = c_hi * c_lo - s_hi * s_lo
        imag = -(s_hi * c_lo + c_hi * s_lo)
        table[g * 2 * own : (g + 1) * 2 * own] = jnp.concatenate([real, imag], axis=0).astype(
            jnp.bfloat16
        )


def dft_table(angles, own, dests, group, frame_len):
    high = pl.BlockSpec((group, frame_len), lambda i: (i, 0))
    low = pl.BlockSpec((own, frame_len), lambda i: (0, 0))
    return pl.pallas_call(
        functools.partial(table_kernel, own),
        grid=(dests // group,),
        in_specs=[high, high, low, low],
        out_specs=pl.BlockSpec((group * 2 * own, frame_len), lambda i: (i, 0)),
        out_shape=jax.ShapeDtypeStruct((dests * 2 * own, frame_len), jnp.bfloat16),
        compiler_params=pltpu.CompilerParams(vmem_limit_bytes=VMEM_LIMIT),
        cost_estimate=pl.CostEstimate(
            flops=dests * own * frame_len * 8,
            bytes_accessed=dests * own * frame_len * 4,
            transcendentals=0,
        ),
    )(*angles)


def dft_kernel(own, table, weighted, pick, spec, power):
    group = spec.shape[0]
    out = lax.dot_general(
        table[...], weighted[...], (((1,), (1,)), ((), ())), preferred_element_type=jnp.float32
    )
    out = out.astype(jnp.bfloat16).reshape(group, 2 * own, out.shape[1])
    spec[...] = out
    values = out.astype(jnp.float32)
    values = values * values
    total = (values[:, :own] + values[:, own:]).reshape(group * own, out.shape[2])
    power[...] = lax.dot_general(
        pick[...],
        total,
        (((1,), (1,)), ((), ())),
        precision=lax.Precision.HIGHEST,
        preferred_element_type=jnp.float32,
    )


def channelise(table, weighted, own, frames, dests, group, limit):
    rows, frame_len = weighted.shape
    column = jnp.arange(rows, dtype=jnp.int32) // (rows // frames)
    pick = (column[None, :] == jnp.arange(frames, dtype=jnp.int32)[:, None]).astype(jnp.float32)
    return pl.pallas_call(
        functools.partial(dft_kernel, own),
        grid=(dests // group,),
        in_specs=[
            pl.BlockSpec((group * 2 * own, frame_len), lambda i: (i, 0)),
            pl.BlockSpec((rows, frame_len), lambda i: (0, 0)),
            pl.BlockSpec((frames, rows), lambda i: (0, 0)),
        ],
        out_specs=[
            pl.BlockSpec((group, 2 * own, rows), lambda i: (i, 0, 0)),
            pl.BlockSpec((frames, group * own), lambda i: (0, i)),
        ],
        out_shape=[
            jax.ShapeDtypeStruct((dests, 2 * own, rows), jnp.bfloat16),
            jax.ShapeDtypeStruct((frames, dests * own), jnp.float32),
        ],
        compiler_params=pltpu.CompilerParams(vmem_limit_bytes=limit),
        cost_estimate=pl.CostEstimate(
            flops=4 * dests * own * frame_len * rows,
            bytes_accessed=dests * own * frame_len * 4,
            transcendentals=0,
        ),
    )(table, weighted, pick)


def channel_rows(wide, channel, stations, blocks, own, local):
    chunks = wide.shape[0] // stations
    slots = 128 // local
    rows = 2 * blocks
    lane = lax.broadcasted_iota(jnp.int32, (rows, 128), 1) // local
    sign = jnp.where(
        lax.broadcasted_iota(jnp.int32, (rows, stations * local), 0) < blocks, 1.0, -1.0
    )
    flat, turned = [], []
    for j in range(chunks):
        halves = []
        for h in range(stations // slots):
            parts = [
                wide[(h * slots + s) * chunks + j, pl.ds(channel, rows, stride=own), :]
                for s in range(slots)
            ]
            tiles = []
            for t in range(slots):
                tile = None
                for s in range(slots):
                    shift = (s - t) % slots * local
                    moved = parts[s] if shift == 0 else pltpu.roll(parts[s], shift, 1)
                    tile = moved if tile is None else jnp.where(lane == s, moved, tile)
                tiles.append(tile)
            halves.append(tiles)
        for t in range(slots):
            full = jnp.concatenate([half[t] for half in halves], axis=1)
            flat.append(full)
            turned.append(pltpu.roll(full, blocks, 0) * sign)
    flat = jnp.concatenate(flat, axis=0).astype(jnp.bfloat16)
    turned = jnp.concatenate(turned, axis=0).astype(jnp.bfloat16)
    return flat, turned


def spread(got, wide, stations, blocks, own):
    chunks = got.shape[2] // 128

    def fill(s, carry):
        for tm in range(blocks):
            for p in range(2):
                piece = got[s * blocks + tm, p * own : (p + 1) * own, :].astype(jnp.float32)
                base = (p * blocks + tm) * own
                for j in range(chunks):
                    wide[s * chunks + j, base : base + own, :] = piece[:, j * 128 : (j + 1) * 128]
        return carry

    lax.fori_loop(0, stations, fill, 0)


def arrange_kernel(stations, blocks, own, local, got, both, wide):
    step = pl.program_id(0)
    group = both.shape[0]
    pl.when(step == 0)(lambda: spread(got, wide, stations, blocks, own))
    for g in range(group):
        pair = channel_rows(wide, step * group + g, stations, blocks, own, local)
        both[g] = jnp.concatenate(pair, axis=1)


def correlate_kernel(stations, blocks, own, local, scale, got, late, vis, wide):
    step = pl.program_id(0)
    group = vis.shape[0]
    inputs = stations * local
    pl.when(step == 0)(lambda: spread(got, wide, stations, blocks, own))
    for g in range(group):
        pair = channel_rows(wide, step * group + g, stations, blocks, own, local)
        both = jnp.concatenate([jnp.concatenate(pair, axis=1), late[g]], axis=0)
        out = lax.dot_general(
            both[:, :inputs],
            both,
            (((0,), (0,)), ((), ())),
            preferred_element_type=jnp.float32,
        )
        vis[g, 0] = out[:, :inputs] * scale
        vis[g, 1] = out[:, inputs:] * scale


def arrange(got, stations, blocks, own, local):
    inputs = stations * local
    depth = got.shape[2] // local * blocks * 2
    group = math.gcd(own, 4)
    return pl.pallas_call(
        functools.partial(arrange_kernel, stations, blocks, own, local),
        grid=(own // group,),
        in_specs=[pl.BlockSpec(memory_space=pltpu.VMEM)],
        out_specs=pl.BlockSpec((group, depth, 2 * inputs), lambda c: (c, 0, 0)),
        out_shape=jax.ShapeDtypeStruct((own, depth, 2 * inputs), jnp.bfloat16),
        scratch_shapes=[
            pltpu.VMEM((stations * got.shape[2] // 128, 2 * blocks * own, 128), jnp.float32)
        ],
        compiler_params=pltpu.CompilerParams(vmem_limit_bytes=VMEM_LIMIT),
        cost_estimate=pl.CostEstimate(
            flops=got.size * 100, bytes_accessed=got.size * 12, transcendentals=0
        ),
    )(got)


def correlate(got, late, stations, blocks, own, local, scale):
    inputs = stations * local
    group = math.gcd(own, 2)
    return pl.pallas_call(
        functools.partial(correlate_kernel, stations, blocks, own, local, scale),
        grid=(own // group,),
        in_specs=[
            pl.BlockSpec(memory_space=pltpu.VMEM),
            pl.BlockSpec((group,) + late.shape[1:], lambda c: (c, 0, 0)),
        ],
        out_specs=pl.BlockSpec((group, 2, inputs, inputs), lambda c: (c, 0, 0, 0)),
        out_shape=jax.ShapeDtypeStruct((own, 2, inputs, inputs), jnp.float32),
        scratch_shapes=[
            pltpu.VMEM((stations * got.shape[2] // 128, 2 * blocks * own, 128), jnp.float32)
        ],
        compiler_params=pltpu.CompilerParams(vmem_limit_bytes=VMEM_LIMIT),
    )(got, late)


def sum_scatter(rows):
    count = rows.shape[0]
    me = lax.axis_index("station")
    distance = count // 2
    while distance > 0:
        upper = me // distance % 2 == 1
        low, high = rows[:distance], rows[distance:]
        route = [(i, i ^ distance) for i in range(count)]
        other = lax.ppermute(jnp.where(upper, low, high), "station", route)
        rows = jnp.where(upper, high, low) + other
        distance //= 2
    return rows[0]


def body(samples, history, taps):
    frames_dev, local, frame_len = samples.shape
    span = taps.shape[0] - 1
    stations, blocks = lax.axis_size("station"), lax.axis_size("tm")
    dests = stations * blocks
    own = frame_len // 2 // dests
    group = max(1, min(dests, 512 // (2 * own)))
    half = frames_dev // 2
    first = lax.axis_index("tm") == 0
    tail = samples[frames_dev - span :]

    near = passed_along(tail[half:], "tm", 1)
    angles = angle_tables(dests, own, frame_len) + angle_tables(own, 1, frame_len)
    table = dft_table(angles, own, dests, group, frame_len)
    own_late = filter_frames(padded(samples, span - half, 0), taps, half)
    near, far_tail, table, own_late = lax.optimization_barrier(
        (near, tail[:half], table, own_late)
    )
    far = passed_along(far_tail, "tm", 1)
    near = jnp.where(first, history[half:], near)
    late = own_late + filter_frames(padded(near, 0, half), taps, half, half + 1)
    late = late.astype(jnp.bfloat16).reshape(half * local, frame_len)
    own_early = filter_frames(
        padded(jnp.concatenate([near, samples[:half]], axis=0), half, 0), taps, half
    )
    late, own_early = lax.optimization_barrier((late, own_early))
    spec_late, power_late = channelise(
        table, late, own, half, dests, group, VMEM_LIMIT
    )
    got_late = lax.all_to_all(spec_late, BOTH, split_axis=0, concat_axis=0, tiled=True)

    far, spec_late, power_late = lax.optimization_barrier((far, spec_late, power_late))
    far = jnp.where(first, history[:half], far)
    early = own_early + filter_frames(
        padded(far, 0, span - half), taps, half, span - half + 1
    )
    early = early.astype(jnp.bfloat16).reshape(half * local, frame_len)
    spec_early, power_early = channelise(
        table, early, own, half, dests, group, 4 * VMEM_LIMIT
    )
    got_late, spec_early, power_early = lax.optimization_barrier(
        (got_late, spec_early, power_early)
    )
    got_early = lax.all_to_all(spec_early, BOTH, split_axis=0, concat_axis=0, tiled=True)

    power = jnp.concatenate([power_early, power_late], axis=0)
    power = sum_scatter(power.reshape(frames_dev, stations, blocks * own).transpose(1, 0, 2))
    power = power * (1.0 / (stations * local))
    scale = 1.0 / (frames_dev * blocks)
    arranged = arrange(got_late, stations, blocks, own, local)
    visibility = correlate(got_early, arranged, stations, blocks, own, local, scale)
    return visibility, power


def solution(mesh):
    return jax.shard_map(
        body,
        mesh=mesh,
        in_specs=(P("tm", "station", None), P(None, "station", None), P()),
        out_specs=(P(("station", "tm"), None, None, None), P("tm", "station")),
        check_vma=False,
    )
```

```python
import functools
import math

import jax
import jax.numpy as jnp
from jax import lax
from jax.experimental import pallas as pl
from jax.experimental.pallas import tpu as pltpu
from jax.sharding import PartitionSpec as P

BOTH = ("station", "tm")
VMEM_LIMIT = 24 * 1024 * 1024


def passed_along(block, axis, distance):
    devices = range(lax.axis_size(axis))
    route = [(i - distance, i) for i in devices if i - distance in devices]
    return lax.ppermute(block, axis, route)


def angle_tables(rows, step, frame_len):
    row = jnp.arange(rows, dtype=jnp.int32) * step
    sample = jnp.arange(frame_len, dtype=jnp.int32)
    phases = row[:, None] * sample[None, :] % frame_len
    angles = phases.astype(jnp.float32) * (2.0 * math.pi / frame_len)
    return jnp.cos(angles), jnp.sin(angles)


def filter_frames(extended, taps, frames_out):
    span_taps = taps.shape[0]
    running = jnp.zeros((frames_out,) + extended.shape[1:], jnp.float32)
    for tap_index in range(span_taps):
        offset = span_taps - 1 - tap_index
        running = running + taps[tap_index][None, None, :] * extended[
            offset : offset + frames_out
        ].astype(jnp.float32)
    return running.astype(jnp.bfloat16)


def table_kernel(own, cos_hi, sin_hi, cos_lo, sin_lo, table):
    c_lo, s_lo = cos_lo[...], sin_lo[...]
    for g in range(cos_hi.shape[0]):
        c_hi, s_hi = cos_hi[g : g + 1], sin_hi[g : g + 1]
        real = c_hi * c_lo - s_hi * s_lo
        imag = -(s_hi * c_lo + c_hi * s_lo)
        table[g * 2 * own : (g + 1) * 2 * own] = jnp.concatenate([real, imag], axis=0).astype(
            jnp.bfloat16
        )


def dft_table(own, dests, group, frame_len):
    cos_hi, sin_hi = angle_tables(dests, own, frame_len)
    cos_lo, sin_lo = angle_tables(own, 1, frame_len)
    high = pl.BlockSpec((group, frame_len), lambda i: (i, 0))
    low = pl.BlockSpec((own, frame_len), lambda i: (0, 0))
    return pl.pallas_call(
        functools.partial(table_kernel, own),
        grid=(dests // group,),
        in_specs=[high, high, low, low],
        out_specs=pl.BlockSpec((group * 2 * own, frame_len), lambda i: (i, 0)),
        out_shape=jax.ShapeDtypeStruct((dests * 2 * own, frame_len), jnp.bfloat16),
        compiler_params=pltpu.CompilerParams(vmem_limit_bytes=VMEM_LIMIT),
        cost_estimate=pl.CostEstimate(
            flops=dests * own * frame_len * 8,
            bytes_accessed=dests * own * frame_len * 4,
            transcendentals=0,
        ),
    )(cos_hi, sin_hi, cos_lo, sin_lo)


def dft_kernel(own, table, weighted, pick, spec, power):
    group = spec.shape[0]
    out = lax.dot_general(
        table[...], weighted[...], (((1,), (1,)), ((), ())), preferred_element_type=jnp.float32
    )
    out = out.astype(jnp.bfloat16).reshape(group, 2 * own, out.shape[1])
    spec[...] = out
    values = out.astype(jnp.float32)
    values = values * values
    total = (values[:, :own] + values[:, own:]).reshape(group * own, out.shape[2])
    power[...] = lax.dot_general(
        pick[...],
        total,
        (((1,), (1,)), ((), ())),
        precision=lax.Precision.HIGHEST,
        preferred_element_type=jnp.float32,
    )


def channelise(table, weighted, own, frames, dests, group):
    rows, frame_len = weighted.shape
    column = jnp.arange(rows, dtype=jnp.int32) // (rows // frames)
    pick = (column[None, :] == jnp.arange(frames, dtype=jnp.int32)[:, None]).astype(jnp.float32)
    return pl.pallas_call(
        functools.partial(dft_kernel, own),
        grid=(dests // group,),
        in_specs=[
            pl.BlockSpec((group * 2 * own, frame_len), lambda i: (i, 0)),
            pl.BlockSpec((rows, frame_len), lambda i: (0, 0)),
            pl.BlockSpec((frames, rows), lambda i: (0, 0)),
        ],
        out_specs=[
            pl.BlockSpec((group, 2 * own, rows), lambda i: (i, 0, 0)),
            pl.BlockSpec((frames, group * own), lambda i: (0, i)),
        ],
        out_shape=[
            jax.ShapeDtypeStruct((dests, 2 * own, rows), jnp.bfloat16),
            jax.ShapeDtypeStruct((frames, dests * own), jnp.float32),
        ],
        compiler_params=pltpu.CompilerParams(vmem_limit_bytes=VMEM_LIMIT),
        cost_estimate=pl.CostEstimate(
            flops=4 * dests * own * frame_len * rows,
            bytes_accessed=dests * own * frame_len * 4,
            transcendentals=0,
        ),
    )(table, weighted, pick)


def channel_rows(wide, channel, stations, blocks, own, local):
    chunks = wide.shape[0] // stations
    slots = 128 // local
    rows = 2 * blocks
    lane = lax.broadcasted_iota(jnp.int32, (rows, 128), 1) // local
    sign = jnp.where(
        lax.broadcasted_iota(jnp.int32, (rows, stations * local), 0) < blocks, 1.0, -1.0
    )
    flat, turned = [], []
    for j in range(chunks):
        halves = []
        for h in range(stations // slots):
            parts = [
                wide[(h * slots + s) * chunks + j, pl.ds(channel, rows, stride=own), :]
                for s in range(slots)
            ]
            tiles = []
            for t in range(slots):
                tile = None
                for s in range(slots):
                    shift = (s - t) % slots * local
                    moved = parts[s] if shift == 0 else pltpu.roll(parts[s], shift, 1)
                    tile = moved if tile is None else jnp.where(lane == s, moved, tile)
                tiles.append(tile)
            halves.append(tiles)
        for t in range(slots):
            full = jnp.concatenate([half[t] for half in halves], axis=1)
            flat.append(full)
            turned.append(pltpu.roll(full, blocks, 0) * sign)
    flat = jnp.concatenate(flat, axis=0).astype(jnp.bfloat16)
    turned = jnp.concatenate(turned, axis=0).astype(jnp.bfloat16)
    return flat, turned


def spread(got, wide, stations, blocks, own):
    chunks = got.shape[2] // 128

    def fill(s, carry):
        for tm in range(blocks):
            for p in range(2):
                piece = got[s * blocks + tm, p * own : (p + 1) * own, :].astype(jnp.float32)
                base = (p * blocks + tm) * own
                for j in range(chunks):
                    wide[s * chunks + j, base : base + own, :] = piece[:, j * 128 : (j + 1) * 128]
        return carry

    lax.fori_loop(0, stations, fill, 0)


def arrange_kernel(stations, blocks, own, local, got, both, wide):
    step = pl.program_id(0)
    group = both.shape[0]
    pl.when(step == 0)(lambda: spread(got, wide, stations, blocks, own))
    for g in range(group):
        pair = channel_rows(wide, step * group + g, stations, blocks, own, local)
        both[g] = jnp.concatenate(pair, axis=1)


def correlate_kernel(stations, blocks, own, local, scale, got, late, vis, wide):
    step = pl.program_id(0)
    group = vis.shape[0]
    inputs = stations * local
    pl.when(step == 0)(lambda: spread(got, wide, stations, blocks, own))
    for g in range(group):
        pair = channel_rows(wide, step * group + g, stations, blocks, own, local)
        both = jnp.concatenate([jnp.concatenate(pair, axis=1), late[g]], axis=0)
        out = lax.dot_general(
            both[:, :inputs],
            both,
            (((0,), (0,)), ((), ())),
            preferred_element_type=jnp.float32,
        )
        vis[g, 0] = out[:, :inputs] * scale
        vis[g, 1] = out[:, inputs:] * scale


def arrange(got, stations, blocks, own, local):
    inputs = stations * local
    depth = got.shape[2] // local * blocks * 2
    group = math.gcd(own, 4)
    return pl.pallas_call(
        functools.partial(arrange_kernel, stations, blocks, own, local),
        grid=(own // group,),
        in_specs=[pl.BlockSpec(memory_space=pltpu.VMEM)],
        out_specs=pl.BlockSpec((group, depth, 2 * inputs), lambda c: (c, 0, 0)),
        out_shape=jax.ShapeDtypeStruct((own, depth, 2 * inputs), jnp.bfloat16),
        scratch_shapes=[
            pltpu.VMEM((stations * got.shape[2] // 128, 2 * blocks * own, 128), jnp.float32)
        ],
        compiler_params=pltpu.CompilerParams(vmem_limit_bytes=VMEM_LIMIT),
        cost_estimate=pl.CostEstimate(
            flops=got.size * 100, bytes_accessed=got.size * 12, transcendentals=0
        ),
    )(got)


def correlate(got, late, stations, blocks, own, local, scale):
    inputs = stations * local
    group = math.gcd(own, 8)
    return pl.pallas_call(
        functools.partial(correlate_kernel, stations, blocks, own, local, scale),
        grid=(own // group,),
        in_specs=[
            pl.BlockSpec(memory_space=pltpu.VMEM),
            pl.BlockSpec((group,) + late.shape[1:], lambda c: (c, 0, 0)),
        ],
        out_specs=pl.BlockSpec((group, 2, inputs, inputs), lambda c: (c, 0, 0, 0)),
        out_shape=jax.ShapeDtypeStruct((own, 2, inputs, inputs), jnp.float32),
        scratch_shapes=[
            pltpu.VMEM((stations * got.shape[2] // 128, 2 * blocks * own, 128), jnp.float32)
        ],
        compiler_params=pltpu.CompilerParams(vmem_limit_bytes=VMEM_LIMIT),
    )(got, late)


def sum_scatter(rows):
    count = rows.shape[0]
    me = lax.axis_index("station")
    distance = count // 2
    while distance > 0:
        upper = me // distance % 2 == 1
        low, high = rows[:distance], rows[distance:]
        route = [(i, i ^ distance) for i in range(count)]
        other = lax.ppermute(jnp.where(upper, low, high), "station", route)
        rows = jnp.where(upper, high, low) + other
        distance //= 2
    return rows[0]


def body(samples, history, taps):
    frames_dev, local, frame_len = samples.shape
    span = taps.shape[0] - 1
    stations, blocks = lax.axis_size("station"), lax.axis_size("tm")
    dests = stations * blocks
    own = frame_len // 2 // dests
    group = max(1, min(dests, 512 // (2 * own)))
    half = frames_dev // 2
    first = lax.axis_index("tm") == 0
    tail = samples[frames_dev - span :]

    near = passed_along(tail[half:], "tm", 1)
    table = dft_table(own, dests, group, frame_len)
    near, far_tail, table = lax.optimization_barrier((near, tail[:half], table))
    far = passed_along(far_tail, "tm", 1)
    near = jnp.where(first, history[half:], near)
    late = filter_frames(jnp.concatenate([near, samples], axis=0), taps, half)
    late = late.reshape(half * local, frame_len)
    spec_late, power_late = channelise(table, late, own, half, dests, group)
    got_late = lax.all_to_all(spec_late, BOTH, split_axis=0, concat_axis=0, tiled=True)

    far = jnp.where(first, history[:half], far)
    early = filter_frames(jnp.concatenate([far, near, samples[:half]], axis=0), taps, half)
    early = early.reshape(half * local, frame_len)
    spec_early, power_early = channelise(table, early, own, half, dests, group)
    got_late, spec_early, power_early = lax.optimization_barrier(
        (got_late, spec_early, power_early)
    )
    got_early = lax.all_to_all(spec_early, BOTH, split_axis=0, concat_axis=0, tiled=True)

    power = jnp.concatenate([power_early, power_late], axis=0)
    power = sum_scatter(power.reshape(frames_dev, stations, blocks * own).transpose(1, 0, 2))
    power = power * (1.0 / (stations * local))
    scale = 1.0 / (frames_dev * blocks)
    arranged = arrange(got_late, stations, blocks, own, local)
    visibility = correlate(got_early, arranged, stations, blocks, own, local, scale)
    return visibility, power


def solution(mesh):
    return jax.shard_map(
        body,
        mesh=mesh,
        in_specs=(P("tm", "station", None), P(None, "station", None), P()),
        out_specs=(P(("station", "tm"), None, None, None), P("tm", "station")),
        check_vma=False,
    )
```

```python
import functools
import math

import jax
import jax.numpy as jnp
from jax import lax
from jax.experimental import pallas as pl
from jax.experimental.pallas import tpu as pltpu
from jax.sharding import PartitionSpec as P

BOTH = ("station", "tm")
VMEM_LIMIT = 24 * 1024 * 1024


def passed_along(block, axis, distance):
    devices = range(lax.axis_size(axis))
    route = [(i - distance, i) for i in devices if i - distance in devices]
    return lax.ppermute(block, axis, route)


def angle_tables(rows, step, frame_len):
    row = jnp.arange(rows, dtype=jnp.int32) * step
    sample = jnp.arange(frame_len, dtype=jnp.int32)
    phases = row[:, None] * sample[None, :] % frame_len
    angles = phases.astype(jnp.float32) * (2.0 * math.pi / frame_len)
    return jnp.cos(angles), jnp.sin(angles)


def filter_frames(extended, taps, frames_out, first_tap=0):
    span_taps = taps.shape[0]
    running = jnp.zeros((frames_out,) + extended.shape[1:], jnp.float32)
    for tap_index in range(first_tap, span_taps):
        offset = span_taps - 1 - tap_index
        running = running + taps[tap_index][None, None, :] * extended[
            offset : offset + frames_out
        ].astype(jnp.float32)
    return running


def padded(frames, before, after):
    return jnp.pad(frames, ((before, after), (0, 0), (0, 0)))


def table_kernel(own, cos_hi, sin_hi, cos_lo, sin_lo, table):
    c_lo, s_lo = cos_lo[...], sin_lo[...]
    for g in range(cos_hi.shape[0]):
        c_hi, s_hi = cos_hi[g : g + 1], sin_hi[g : g + 1]
        real = c_hi * c_lo - s_hi * s_lo
        imag = -(s_hi * c_lo + c_hi * s_lo)
        table[g * 2 * own : (g + 1) * 2 * own] = jnp.concatenate([real, imag], axis=0).astype(
            jnp.bfloat16
        )


def dft_table(own, dests, group, frame_len):
    cos_hi, sin_hi = angle_tables(dests, own, frame_len)
    cos_lo, sin_lo = angle_tables(own, 1, frame_len)
    high = pl.BlockSpec((group, frame_len), lambda i: (i, 0))
    low = pl.BlockSpec((own, frame_len), lambda i: (0, 0))
    return pl.pallas_call(
        functools.partial(table_kernel, own),
        grid=(dests // group,),
        in_specs=[high, high, low, low],
        out_specs=pl.BlockSpec((group * 2 * own, frame_len), lambda i: (i, 0)),
        out_shape=jax.ShapeDtypeStruct((dests * 2 * own, frame_len), jnp.bfloat16),
        compiler_params=pltpu.CompilerParams(vmem_limit_bytes=VMEM_LIMIT),
        cost_estimate=pl.CostEstimate(
            flops=dests * own * frame_len * 8,
            bytes_accessed=dests * own * frame_len * 4,
            transcendentals=0,
        ),
    )(cos_hi, sin_hi, cos_lo, sin_lo)


def dft_kernel(own, table, weighted, pick, spec, power):
    group = spec.shape[0]
    out = lax.dot_general(
        table[...], weighted[...], (((1,), (1,)), ((), ())), preferred_element_type=jnp.float32
    )
    out = out.astype(jnp.bfloat16).reshape(group, 2 * own, out.shape[1])
    spec[...] = out
    values = out.astype(jnp.float32)
    values = values * values
    total = (values[:, :own] + values[:, own:]).reshape(group * own, out.shape[2])
    power[...] = lax.dot_general(
        pick[...],
        total,
        (((1,), (1,)), ((), ())),
        precision=lax.Precision.HIGHEST,
        preferred_element_type=jnp.float32,
    )


def channelise(table, weighted, own, frames, dests, group, limit):
    rows, frame_len = weighted.shape
    column = jnp.arange(rows, dtype=jnp.int32) // (rows // frames)
    pick = (column[None, :] == jnp.arange(frames, dtype=jnp.int32)[:, None]).astype(jnp.float32)
    return pl.pallas_call(
        functools.partial(dft_kernel, own),
        grid=(dests // group,),
        in_specs=[
            pl.BlockSpec((group * 2 * own, frame_len), lambda i: (i, 0)),
            pl.BlockSpec((rows, frame_len), lambda i: (0, 0)),
            pl.BlockSpec((frames, rows), lambda i: (0, 0)),
        ],
        out_specs=[
            pl.BlockSpec((group, 2 * own, rows), lambda i: (i, 0, 0)),
            pl.BlockSpec((frames, group * own), lambda i: (0, i)),
        ],
        out_shape=[
            jax.ShapeDtypeStruct((dests, 2 * own, rows), jnp.bfloat16),
            jax.ShapeDtypeStruct((frames, dests * own), jnp.float32),
        ],
        compiler_params=pltpu.CompilerParams(vmem_limit_bytes=limit),
        cost_estimate=pl.CostEstimate(
            flops=4 * dests * own * frame_len * rows,
            bytes_accessed=dests * own * frame_len * 4,
            transcendentals=0,
        ),
    )(table, weighted, pick)


def channel_rows(wide, channel, stations, blocks, own, local):
    chunks = wide.shape[0] // stations
    slots = 128 // local
    rows = 2 * blocks
    lane = lax.broadcasted_iota(jnp.int32, (rows, 128), 1) // local
    sign = jnp.where(
        lax.broadcasted_iota(jnp.int32, (rows, stations * local), 0) < blocks, 1.0, -1.0
    )
    flat, turned = [], []
    for j in range(chunks):
        halves = []
        for h in range(stations // slots):
            parts = [
                wide[(h * slots + s) * chunks + j, pl.ds(channel, rows, stride=own), :]
                for s in range(slots)
            ]
            tiles = []
            for t in range(slots):
                tile = None
                for s in range(slots):
                    shift = (s - t) % slots * local
                    moved = parts[s] if shift == 0 else pltpu.roll(parts[s], shift, 1)
                    tile = moved if tile is None else jnp.where(lane == s, moved, tile)
                tiles.append(tile)
            halves.append(tiles)
        for t in range(slots):
            full = jnp.concatenate([half[t] for half in halves], axis=1)
            flat.append(full)
            turned.append(pltpu.roll(full, blocks, 0) * sign)
    flat = jnp.concatenate(flat, axis=0).astype(jnp.bfloat16)
    turned = jnp.concatenate(turned, axis=0).astype(jnp.bfloat16)
    return flat, turned


def spread(got, wide, stations, blocks, own):
    chunks = got.shape[2] // 128

    def fill(s, carry):
        for tm in range(blocks):
            for p in range(2):
                piece = got[s * blocks + tm, p * own : (p + 1) * own, :].astype(jnp.float32)
                base = (p * blocks + tm) * own
                for j in range(chunks):
                    wide[s * chunks + j, base : base + own, :] = piece[:, j * 128 : (j + 1) * 128]
        return carry

    lax.fori_loop(0, stations, fill, 0)


def arrange_kernel(stations, blocks, own, local, got, both, wide):
    step = pl.program_id(0)
    group = both.shape[0]
    pl.when(step == 0)(lambda: spread(got, wide, stations, blocks, own))
    for g in range(group):
        pair = channel_rows(wide, step * group + g, stations, blocks, own, local)
        both[g] = jnp.concatenate(pair, axis=1)


def correlate_kernel(stations, blocks, own, local, scale, got, late, vis, wide):
    step = pl.program_id(0)
    group = vis.shape[0]
    inputs = stations * local
    pl.when(step == 0)(lambda: spread(got, wide, stations, blocks, own))
    for g in range(group):
        pair = channel_rows(wide, step * group + g, stations, blocks, own, local)
        both = jnp.concatenate([jnp.concatenate(pair, axis=1), late[g]], axis=0)
        out = lax.dot_general(
            both[:, :inputs],
            both,
            (((0,), (0,)), ((), ())),
            preferred_element_type=jnp.float32,
        )
        vis[g, 0] = out[:, :inputs] * scale
        vis[g, 1] = out[:, inputs:] * scale


def arrange(got, stations, blocks, own, local):
    inputs = stations * local
    depth = got.shape[2] // local * blocks * 2
    group = math.gcd(own, 4)
    return pl.pallas_call(
        functools.partial(arrange_kernel, stations, blocks, own, local),
        grid=(own // group,),
        in_specs=[pl.BlockSpec(memory_space=pltpu.VMEM)],
        out_specs=pl.BlockSpec((group, depth, 2 * inputs), lambda c: (c, 0, 0)),
        out_shape=jax.ShapeDtypeStruct((own, depth, 2 * inputs), jnp.bfloat16),
        scratch_shapes=[
            pltpu.VMEM((stations * got.shape[2] // 128, 2 * blocks * own, 128), jnp.float32)
        ],
        compiler_params=pltpu.CompilerParams(vmem_limit_bytes=VMEM_LIMIT),
        cost_estimate=pl.CostEstimate(
            flops=got.size * 100, bytes_accessed=got.size * 12, transcendentals=0
        ),
    )(got)


def correlate(got, late, stations, blocks, own, local, scale):
    inputs = stations * local
    group = math.gcd(own, 8)
    return pl.pallas_call(
        functools.partial(correlate_kernel, stations, blocks, own, local, scale),
        grid=(own // group,),
        in_specs=[
            pl.BlockSpec(memory_space=pltpu.VMEM),
            pl.BlockSpec((group,) + late.shape[1:], lambda c: (c, 0, 0)),
        ],
        out_specs=pl.BlockSpec((group, 2, inputs, inputs), lambda c: (c, 0, 0, 0)),
        out_shape=jax.ShapeDtypeStruct((own, 2, inputs, inputs), jnp.float32),
        scratch_shapes=[
            pltpu.VMEM((stations * got.shape[2] // 128, 2 * blocks * own, 128), jnp.float32)
        ],
        compiler_params=pltpu.CompilerParams(vmem_limit_bytes=VMEM_LIMIT),
    )(got, late)


def sum_scatter(rows):
    count = rows.shape[0]
    me = lax.axis_index("station")
    distance = count // 2
    while distance > 0:
        upper = me // distance % 2 == 1
        low, high = rows[:distance], rows[distance:]
        route = [(i, i ^ distance) for i in range(count)]
        other = lax.ppermute(jnp.where(upper, low, high), "station", route)
        rows = jnp.where(upper, high, low) + other
        distance //= 2
    return rows[0]


def body(samples, history, taps):
    frames_dev, local, frame_len = samples.shape
    span = taps.shape[0] - 1
    stations, blocks = lax.axis_size("station"), lax.axis_size("tm")
    dests = stations * blocks
    own = frame_len // 2 // dests
    group = max(1, min(dests, 512 // (2 * own)))
    half = frames_dev // 2
    first = lax.axis_index("tm") == 0
    tail = samples[frames_dev - span :]

    near = passed_along(tail[half:], "tm", 1)
    table = dft_table(own, dests, group, frame_len)
    own_late = filter_frames(padded(samples, span - half, 0), taps, half)
    near, far_tail, table, own_late = lax.optimization_barrier(
        (near, tail[:half], table, own_late)
    )
    far = passed_along(far_tail, "tm", 1)
    near = jnp.where(first, history[half:], near)
    late = own_late + filter_frames(padded(near, 0, half), taps, half, half + 1)
    late = late.astype(jnp.bfloat16).reshape(half * local, frame_len)
    spec_late, power_late = channelise(
        table, late, own, half, dests, group, VMEM_LIMIT
    )
    got_late = lax.all_to_all(spec_late, BOTH, split_axis=0, concat_axis=0, tiled=True)

    far, near, late = lax.optimization_barrier((far, near, late))
    far = jnp.where(first, history[:half], far)
    early = filter_frames(jnp.concatenate([far, near, samples[:half]], axis=0), taps, half)
    early = early.astype(jnp.bfloat16).reshape(half * local, frame_len)
    spec_early, power_early = channelise(
        table, early, own, half, dests, group, 56 * 1024 * 1024
    )
    got_late, spec_early, power_early = lax.optimization_barrier(
        (got_late, spec_early, power_early)
    )
    got_early = lax.all_to_all(spec_early, BOTH, split_axis=0, concat_axis=0, tiled=True)

    power = jnp.concatenate([power_early, power_late], axis=0)
    power = sum_scatter(power.reshape(frames_dev, stations, blocks * own).transpose(1, 0, 2))
    power = power * (1.0 / (stations * local))
    scale = 1.0 / (frames_dev * blocks)
    arranged = arrange(got_late, stations, blocks, own, local)
    visibility = correlate(got_early, arranged, stations, blocks, own, local, scale)
    return visibility, power


def solution(mesh):
    return jax.shard_map(
        body,
        mesh=mesh,
        in_specs=(P("tm", "station", None), P(None, "station", None), P()),
        out_specs=(P(("station", "tm"), None, None, None), P("tm", "station")),
        check_vma=False,
    )
```
